32 devices in a mesh: group: 2 (over y), freq: 4 (over z), shot: 2 (over x), half: 2 (over core).
Axes of the slice: x: 2, y: 2, z: 4, core: 2. Of those that a mesh axis runs over, the one named last changes fastest.
Arguments:
- records: bfloat16 [8, 64, 128, 512], P(('group', 'shot'), 'half', 'freq'), parts along dimension 0, may hold values from -6 to 6
- source_pattern: bfloat16 [8, 64, 128], P(('group', 'shot'), 'half'), parts along dimension 0, may hold values from -6 to 6
- wavelet: float32 [256, 2], replicated, may hold values from -6 to 6
- filters: bfloat16 [2, 2, 13, 13, 256], replicated, may hold values from -0.3125 to 0.3125
- vel_table: float32 [64], replicated, may hold values from 0 to 1
- vel_index: int32 [4, 64, 128], P('group', 'half'), parts along dimension 0, may hold values from 0 to 63
- freq_plan: int32 [4, 6], replicated, may hold values from 0 to 255, as said below
- counts: int32 [4], replicated, may hold values from 1 to 6, 12 in all
Outputs:
- image: float32 [2, 32, 4, 128], P('half', 'freq', 'group'), parts along dimension 2
The draws below stay inside these ranges and needn't reach their ends.
There are 2 independent parts, one for each index of `group`. The reference program is written for one: setup_inputs(seed, part) draws one part's arguments, and reference() takes and returns one part's arrays. A program takes and returns all parts, laid end to end along the dimension named above; an argument that names none is the same for every part. Nothing has to cross between parts.
Inputs may be any that keep to these rules, and one draw needn't show every extreme that they name: `freq_plan`: entries are distinct bins; 0 and 255 both appear. `counts`: they sum to 12; the largest is exactly 6.
All inputs are finite; a program needn't handle non-finite values.
Results may differ from the reference program's by a relative error of at most 0.0069.
Values may be sent and summed in bfloat16 or wider, within the bound.
A program may use at most 64 MiB of HBM per device.

```python
import math
import jax
import jax.numpy as jnp
import numpy as np
from jax import lax

ROWS_DEV = 32
NX = 128
NT = 512
DEPTH = 2
TAPS = 13
NREF = 2
NV = 64
NBIN = 256
FCAP = 6
NF = 12
NY = 64
SHOTS = 4
N_FREQ = 4
N_HALF = 2


def draw_freq_plan(key, part):
    slot_total = N_FREQ * FCAP
    order = jax.random.permutation(key, slot_total)
    bin_ids = order * (NBIN - 1) // (slot_total - 1)
    return bin_ids.reshape(N_FREQ, FCAP).astype(jnp.int32)


def touch_ends(result, rng, low, top_value):
    shape = result.shape
    index_at = [jax.random.randint(jax.random.fold_in(rng, axis), (), 0, shape[axis]) for axis in range(len(shape))]
    result = result.at[tuple(index_at)].set(low)
    longest = shape.index(max(shape))
    index_at[longest] = (index_at[longest] + 1) % shape[longest]
    return result.at[tuple(index_at)].set(top_value)


def shard_levels(stream_key, dims, shards, low, top_value):
    def one(dim, blocks):
        heights = jax.random.uniform(jax.random.fold_in(jax.random.fold_in(stream_key, 6), dim), (blocks,), jnp.float32, low / len(shards), top_value / len(shards))
        return jnp.repeat(jnp.exp(heights), dims[dim] // blocks).reshape((-1,) + (1,) * (len(dims) - dim - 1))

    factor_of = one(*shards[0])
    for cut in shards[1:]:
        factor_of = factor_of * one(*cut)
    return factor_of


def profile(amount, total, bound, slope):
    portions = [(1 << 20) // math.isqrt(standing ** slope) + 1 for standing in range(2, amount + 1)]
    surplus, given = total - bound - (amount - 1), [1] * (amount - 1)
    while surplus > 0:
        candidates = [i for i in range(amount - 1) if given[i] < bound]
        pool, left = sum([portions[i] for i in candidates]), surplus
        for i in candidates:
            more = min(bound - given[i], max(1, left * portions[i] // pool), surplus)
            given[i] = given[i] + more
            surplus = surplus - more
    return np.array([bound] + given)


def ragged(key, amount, total, most, skew):
    if amount == 2:
        one = jax.random.randint(key, (), max(1, total - most), min(most, total - 1) + 1)
        return jnp.stack([one, total - one])
    lengths = jnp.asarray(profile(amount, total, most, skew), jnp.int32)
    pairs = (amount - 1) // 2
    donor, taker = lengths[1:1 + 2 * pairs:2], lengths[2:2 + 2 * pairs:2]
    slack = jnp.minimum(donor - 1, most - taker)
    shifted = jax.random.randint(jax.random.fold_in(key, 1), (pairs,), 0, 1 << 20) % (slack + 1)
    lengths = lengths.at[1:1 + 2 * pairs:2].set(donor - shifted).at[2:2 + 2 * pairs:2].set(taker + shifted)
    return lengths[jax.random.permutation(jax.random.fold_in(key, 2), amount)]


def normal_values(stream_key, dims, deviation, most, split=(), kind=jnp.bfloat16):
    result = deviation * jax.random.normal(stream_key, dims, jnp.float32)
    if split:
        result = result * shard_levels(stream_key, dims, split, -0.22, 0.18)
    return jnp.clip(result, -most, most).astype(kind)


def setup_inputs(seed: int = 0, part: int = 0) -> dict:
    arg_keys = jax.random.split(jax.random.key(seed), 9)
    own_keys = jax.random.split(jax.random.fold_in(arg_keys[8], part), 9)
    return {
        "records": normal_values(own_keys[0], (SHOTS, NY, NX, NT), 1.0, 6.0, ((0, 2), (1, 2), (2, 4))),
        "source_pattern": normal_values(own_keys[1], (SHOTS, NY, NX), 1.0, 6.0, ((0, 2), (1, 2))),
        "wavelet": normal_values(arg_keys[2], (NBIN, 2), 1.0, 6.0, (), jnp.float32),
        "filters": normal_values(arg_keys[3], (NREF, 2, TAPS, TAPS, NBIN), (2 * TAPS * TAPS) ** -0.5, 0.3125),
        "vel_table": jnp.clip(jax.random.uniform(arg_keys[4], (NV,), jnp.float32, 0.0, 1.0), 0.0, 1.0),
        "vel_index": touch_ends(jax.random.randint(own_keys[5], (DEPTH, NY, NX), 0, NV), jax.random.fold_in(own_keys[5], 1), 0, NV - 1).astype(jnp.int32),
        "freq_plan": draw_freq_plan(jax.random.fold_in(arg_keys[8], 71), part),
        "counts": ragged(arg_keys[7], N_FREQ, NF, FCAP, 2).astype(jnp.int32),
    }


def live_bins(freq_plan, counts):
    run_ends = jnp.cumsum(counts).astype(jnp.int32)
    starts = run_ends - counts
    global_slot = jnp.arange(NF, dtype=jnp.int32)
    holder = lax.optimization_barrier(jnp.sum((run_ends[None, :] <= global_slot[:, None]).astype(jnp.int32), axis=1))
    offset = global_slot - starts[holder]
    return freq_plan[holder, offset]

def dft_columns(bin_ids):
    sample = jnp.arange(NT, dtype=jnp.int32)
    phases = bin_ids[None, :] * sample[:, None] % NT
    angles = phases.astype(jnp.float32) * (2.0 * math.pi / NT)
    dft_scale = 1.0 / math.sqrt(NT)
    return jnp.stack([jnp.cos(angles) * dft_scale, -jnp.sin(angles) * dft_scale], axis=-1).astype(jnp.bfloat16)

def extrapolate(fields, filter_taps, blends):
    half_taps = TAPS // 2
    row_count = fields.shape[-2]
    col_count = fields.shape[-1]
    padded = jnp.pad(fields.astype(jnp.float32), ((0, 0), (0, 0), (0, 0), (half_taps, half_taps), (half_taps, half_taps)))
    real_acc = jnp.zeros((NREF,) + fields.shape[:2] + (row_count, col_count), jnp.float32)
    imag_acc = jnp.zeros((NREF,) + fields.shape[:2] + (row_count, col_count), jnp.float32)
    for row_shift in range(TAPS):
        for col_shift in range(TAPS):
            window = padded[:, :, :, row_shift:row_shift + row_count, col_shift:col_shift + col_count]
            tap_real = filter_taps[:, 0, row_shift, col_shift][:, None, None, None, None]
            tap_imag = filter_taps[:, 1, row_shift, col_shift][:, None, None, None, None]
            real_acc = real_acc + tap_real * window[None, :, :, 0] - tap_imag * window[None, :, :, 1]
            imag_acc = imag_acc + tap_real * window[None, :, :, 1] + tap_imag * window[None, :, :, 0]
    out_real = real_acc[0] + blends * (real_acc[1] - real_acc[0])
    out_imag = imag_acc[0] + blends * (imag_acc[1] - imag_acc[0])
    return jnp.stack([out_real, out_imag], axis=2).astype(jnp.bfloat16)

def reference(records, source_pattern, wavelet, filters, vel_table, vel_index, freq_plan, counts):
    bin_ids = live_bins(freq_plan, counts)
    dft_table = dft_columns(bin_ids)
    spectra = jnp.dot(records.reshape(-1, NT), dft_table.reshape(NT, NF * 2), preferred_element_type=jnp.float32)
    spectra = spectra.reshape(SHOTS, NY, NX, NF, 2).transpose(3, 0, 4, 1, 2)
    blends = vel_table[vel_index]
    pattern = source_pattern.astype(jnp.float32)

    def migrate(inputs):
        own_spectra, bin_id = inputs
        filter_taps = filters[..., bin_id].astype(jnp.float32)
        wavelet_bin = wavelet[bin_id]
        source = (pattern[:, None] * wavelet_bin[None, :, None, None]).astype(jnp.bfloat16)
        receiver = own_spectra.astype(jnp.bfloat16)
        fields = jnp.stack([source, receiver])
        images = []
        for depth_step in range(DEPTH):
            fields = extrapolate(fields, filter_taps, blends[depth_step])
            as_float = fields.astype(jnp.float32)
            images.append(lax.optimization_barrier(jnp.sum(as_float[0, :, 0] * as_float[1, :, 0] + as_float[0, :, 1] * as_float[1, :, 1], axis=0)))
        return jnp.stack(images)
    per_bin = lax.map(migrate, (spectra, bin_ids))
    image_scale = 1.0 / math.sqrt(NF * SHOTS)
    summed = lax.optimization_barrier(jnp.sum(per_bin, axis=0)) * image_scale
    return summed.transpose(1, 0, 2).reshape(N_HALF, ROWS_DEV, DEPTH, NX)
```

```python
import functools
import math

import jax
import jax.numpy as jnp
from jax import lax
from jax.experimental import pallas as pl
from jax.experimental.pallas import tpu as pltpu
from jax.sharding import PartitionSpec as P

LANES = 128
SUB = 8
SEG = 16
MESH = pl.DeviceIdType.MESH
FPD = 3


def kernel(
    dims,
    records_any, pattern_any, wavelet_any, filters_any, table_any, index_any, plan_any, counts_any,
    out_ref,
    records_ref, pattern_ref, wavelet_ref, filters_ref, table_ref, index_ref, plan_ref, counts_ref,
    send_ref, recv_ref, taps_ref, bands_ref, stack_ref, field0_ref, field1_ref, part_ref, gather_ref,
    load_sem, a2a_send, a2a_recv, halo_send, halo_recv, red_send, red_recv,
):
    groups, shots_axis, planes, rows, own_cols, taps, nref, depth, samples = dims
    half_taps = taps // 2
    pad = half_taps * SUB
    body_rows = rows * SUB
    freq = lax.axis_index("freq")
    shot = lax.axis_index("shot")
    half = lax.axis_index("half")
    members = groups * shots_axis
    me = freq * shots_axis + shot

    barrier = pltpu.get_barrier_semaphore()
    for step in range(1, members):
        other = lax.rem(me + step, members)
        pl.semaphore_signal(
            barrier, inc=1,
            device_id={"freq": other // shots_axis, "shot": lax.rem(other, shots_axis)},
            device_id_type=MESH,
        )
    pl.semaphore_signal(barrier, inc=1, device_id={"half": 1 - half}, device_id_type=MESH)

    loads = []
    for place, (source, target) in enumerate((
        (counts_any, counts_ref), (plan_any, plan_ref), (records_any, records_ref),
        (filters_any, filters_ref), (wavelet_any, wavelet_ref), (table_any, table_ref),
        (index_any, index_ref), (pattern_any, pattern_ref),
    )):
        copy = pltpu.make_async_copy(source, target, load_sem.at[place])
        copy.start()
        loads.append(copy)
    loads[0].wait()
    loads[1].wait()

    slots = plan_ref.shape[1]

    def bin_of(wanted):
        run = jnp.int32(0)
        start = jnp.int32(0)
        holder = jnp.int32(0)
        for group in range(groups):
            run = run + counts_ref[group]
            past = run <= wanted
            holder = holder + past.astype(jnp.int32)
            start = jnp.where(past, run, start)
        holder = jnp.minimum(holder, groups - 1)
        return plan_ref[holder, jnp.minimum(wanted - start, slots - 1)]

    per_group = SUB // 2
    wave_plane = lax.broadcasted_iota(jnp.int32, (SUB, samples), 0) // 2
    wave_part = lax.broadcasted_iota(jnp.int32, (SUB, samples), 0) % 2
    sample = lax.broadcasted_iota(jnp.int32, (SUB, samples), 1)
    waves = []
    for first in range(0, groups * planes, per_group):
        bins = jnp.zeros((SUB, samples), jnp.int32)
        for plane in range(per_group):
            bins = jnp.where(wave_plane == plane, bin_of(jnp.int32(first + plane)), bins)
        phase = (bins * sample + wave_part * (samples // 4)) & (samples - 1)
        waves.append(phase.astype(jnp.float32) * (2.0 * math.pi / samples))
    waves = jnp.concatenate(waves, axis=0) if len(waves) > 1 else waves[0]
    waves = (jnp.cos(waves) * (1.0 / math.sqrt(samples))).astype(jnp.bfloat16)
    table_rows = groups * planes * SUB
    spread_row = lax.broadcasted_iota(jnp.int32, (table_rows, waves.shape[0]), 0)
    spread_col = lax.broadcasted_iota(jnp.int32, (table_rows, waves.shape[0]), 1)
    spread_to = (spread_row // SUB) * 2 + (spread_row % SUB) // (SUB // 2)
    spread_hot = (spread_col == spread_to).astype(jnp.float32).astype(jnp.bfloat16)
    dft = jnp.dot(spread_hot, waves, preferred_element_type=jnp.float32).astype(jnp.bfloat16)

    sub_row = lax.broadcasted_iota(jnp.int32, (SUB, LANES), 0)
    odd_shot = (sub_row & 1) == 1
    second = (sub_row & 2) == 2
    upper = sub_row >= SUB // 2

    half_lanes = rows * own_cols
    loads[2].wait()
    spectra = []
    for index in range(2):
        block = records_ref[index * half_lanes:(index + 1) * half_lanes, :]
        spectra.append(
            lax.dot_general(dft, block, (((1,), (1,)), ((), ())), preferred_element_type=jnp.float32)
        )
    strips = half_lanes // LANES
    pairs = 2 if strips % 2 == 0 else 1
    packs = strips // pairs
    for holder in range(groups):
        for plane in range(planes):
            pieces = []
            base = (holder * planes + plane) * SUB
            for pack in range(packs):
                chosen = []
                for pair in range(pairs):
                    at = (pack * pairs + pair) * LANES
                    chosen.append(
                        jnp.where(
                            odd_shot,
                            spectra[1][base:base + SUB, at:at + LANES],
                            spectra[0][base:base + SUB, at:at + LANES],
                        )
                    )
                pieces.append(chosen[0] if pairs == 1 else jnp.where(second, chosen[1], chosen[0]))
            piece = jnp.concatenate(pieces, axis=0) if packs > 1 else pieces[0]
            send_ref[holder, plane] = piece.astype(jnp.bfloat16)
    recv_ref[freq] = send_ref[freq]

    pl.semaphore_wait(barrier, members)

    exchanges = []
    for plane in range(planes):
        arriving = []
        for step in range(1, groups):
            other = lax.rem(freq + step, groups)
            copy = pltpu.make_async_remote_copy(
                src_ref=send_ref.at[other, plane],
                dst_ref=recv_ref.at[freq, plane],
                send_sem=a2a_send.at[plane, step],
                recv_sem=a2a_recv.at[plane, step],
                device_id={"freq": other},
                device_id_type=MESH,
            )
            copy.start()
            arriving.append(copy)
        exchanges.append(arriving)

    bin_total = taps_ref.shape[1]
    own_bins = [bin_of(freq * planes + plane) for plane in range(planes)]
    segments = nref * taps
    taps_ref[...] = jnp.zeros_like(taps_ref)
    for copy in loads[3:]:
        copy.wait()
    for segment in range(segments):
        for tap in range(taps):
            at = segment * 2 * SEG + 2 * tap
            taps_ref[at:at + 2, :] = filters_ref[segment, tap]
    bin_lane = lax.broadcasted_iota(jnp.int32, (SUB, bin_total), 1)
    bin_row = lax.broadcasted_iota(jnp.int32, (SUB, bin_total), 0)
    wanted_bin = jnp.full((SUB, bin_total), -1, jnp.int32)
    for plane in range(planes):
        wanted_bin = jnp.where(bin_row == plane, own_bins[plane], wanted_bin)
    bin_hot = (wanted_bin == bin_lane).astype(jnp.float32).astype(jnp.bfloat16)
    picked = lax.dot_general(
        bin_hot, taps_ref[...], (((1,), (1,)), ((), ())), preferred_element_type=jnp.float32
    ).astype(jnp.bfloat16)
    lane_in = lax.broadcasted_iota(jnp.int32, (LANES, LANES), 0)
    lane_out = lax.broadcasted_iota(jnp.int32, (LANES, LANES), 1)
    turn = (
        (lane_in // (2 * SEG) == lane_out // (2 * SEG))
        & (lane_in % 2 == (lane_out % (2 * SEG)) // SEG)
        & ((lane_in % (2 * SEG)) // 2 + lane_out % SEG == taps - 1)
    ).astype(jnp.float32).astype(jnp.bfloat16)
    per_tile = LANES // SEG
    turned = []
    for at in range(0, segments * 2 * SEG, LANES):
        width = min(LANES, segments * 2 * SEG - at)
        turned.append(
            jnp.dot(
                picked[:, at:at + width], turn[:width, :], preferred_element_type=jnp.float32
            )
        )
    in_band = (lane_out - lane_in + half_taps >= 0) & (lane_out - lane_in + half_taps < taps)
    for line in range(2 * segments):
        shift = (-(half_taps + (line % per_tile) * SEG)) % LANES
        placed = pltpu.roll(turned[line // per_tile], shift, 1)
        segment = line // 2
        tap_row = segment % taps
        side = (segment // taps) * 2 + line % 2
        for plane in range(planes):
            wide = jnp.broadcast_to(placed[plane:plane + 1, :], (LANES, LANES))
            rolled = pltpu.roll(wide, 0, 1, stride=1, stride_axis=0)
            bands_ref[
                plane, tap_row * LANES:(tap_row + 1) * LANES, side * LANES:(side + 1) * LANES
            ] = jnp.where(in_band, rolled, 0.0).astype(jnp.bfloat16)

    blends = []
    for level in range(depth):
        classes = index_ref[level]
        weight = jnp.zeros(classes.shape, jnp.float32)
        for entry in range(table_ref.shape[0]):
            weight = jnp.where(classes == entry, table_ref[entry], weight)
        blends.append(weight)

    outer = pl.multiple_of(half * (body_rows + pad), SUB)
    for plane in range(planes):
        field0_ref[plane, pl.ds(outer, pad), :] = jnp.zeros((pad, LANES), jnp.float32)
        field1_ref[plane, pl.ds(outer, pad), :] = jnp.zeros((pad, LANES), jnp.float32)
    pattern = [pattern_ref[index].astype(jnp.float32) for index in range(2)]
    wave_lane = lax.broadcasted_iota(jnp.int32, wavelet_ref.shape, 1)
    gains = []
    for plane in range(planes):
        gain = jnp.sum(
            jnp.where(wave_lane == own_bins[plane], wavelet_ref[...], 0.0), axis=1, keepdims=True
        )
        gains.append(
            jnp.where(
                upper,
                jnp.broadcast_to(gain[1:2, :], (SUB, LANES)),
                jnp.broadcast_to(gain[0:1, :], (SUB, LANES)),
            )
        )

    inner = pl.multiple_of(body_rows - half * (body_rows - pad), SUB)
    target = pl.multiple_of(half * (body_rows + pad), SUB)

    def swap(level, plane):
        field_ref = field0_ref if level == 0 else field1_ref
        copy = pltpu.make_async_remote_copy(
            src_ref=field_ref.at[plane, pl.ds(inner, pad), :],
            dst_ref=field_ref.at[plane, pl.ds(target, pad), :],
            send_sem=halo_send.at[level, plane],
            recv_sem=halo_recv.at[level, plane],
            device_id={"half": 1 - half},
            device_id_type=MESH,
        )
        copy.start()
        return copy

    lane = lax.broadcasted_iota(jnp.int32, (packs * SUB, LANES), 1) // own_cols
    strip_rows = LANES // own_cols

    def assemble(plane):
        for copy in exchanges[plane]:
            copy.wait()
        blocks = [recv_ref[group, plane].astype(jnp.float32) for group in range(groups)]
        for low in range(strip_rows):
            merged = jnp.zeros((packs * SUB, LANES), jnp.float32)
            for group in range(groups):
                shift = ((group - low) * own_cols) % LANES
                moved = blocks[group] if shift == 0 else pltpu.roll(blocks[group], shift, 1)
                merged = jnp.where(lane == group, moved, merged)
            for pack in range(packs):
                value = merged[pack * SUB:(pack + 1) * SUB, :]
                for pair in range(pairs):
                    row = (pack * pairs + pair) * strip_rows + low
                    receiver = value
                    if pairs == 2 and pair == 0:
                        receiver = pltpu.roll(value, 2, 0)
                    source = jnp.where(
                        odd_shot, pattern[1][row:row + 1, :], pattern[0][row:row + 1, :]
                    ) * gains[plane]
                    source = source.astype(jnp.bfloat16).astype(jnp.float32)
                    field0_ref[plane, pad + row * SUB:pad + (row + 1) * SUB, :] = jnp.where(
                        second, receiver, source
                    )
        return swap(0, plane)

    row3 = lax.broadcasted_iota(jnp.int32, (rows, SUB, LANES), 1)
    sign = jnp.where(row3 >= SUB // 2, 1.0, -1.0)
    image_row = (row3 & 2) == 0
    share = rows // groups

    def extrapolate(level, plane):
        field_ref = field0_ref if level == 0 else field1_ref
        for tap_row in range(taps):
            stack_ref[:, tap_row * LANES:(tap_row + 1) * LANES] = field_ref[
                plane, tap_row * SUB:tap_row * SUB + body_rows, :
            ].astype(jnp.bfloat16)
        sides = []
        for side in range(nref):
            both = jnp.dot(
                stack_ref[...],
                bands_ref[plane, :, 2 * side * LANES:2 * (side + 1) * LANES],
                preferred_element_type=jnp.float32,
            )
            direct = both[:, :LANES].reshape(rows, SUB, LANES)
            crossed = both[:, LANES:].reshape(rows, SUB, LANES)
            sides.append(direct + sign * pltpu.roll(crossed, SUB // 2, 1))
        value = sides[0] + blends[level][:, None, :] * (sides[1] - sides[0])
        value = value.astype(jnp.bfloat16).astype(jnp.float32)
        copy = None
        if level + 1 < depth:
            field1_ref[plane, pad:pad + body_rows, :] = value.reshape(body_rows, LANES)
            copy = swap(level + 1, plane)
        return value * pltpu.roll(value, SUB - 2, 1), copy

    halos = {}
    ahead = min(2, planes)
    for plane in range(ahead):
        halos[plane] = assemble(plane)
    reductions = []
    for level in range(depth):
        total = jnp.zeros((rows, SUB, LANES), jnp.float32)
        following = {}
        for plane in range(planes):
            halos[plane].wait()
            term, following[plane] = extrapolate(level, plane)
            total = total + term
            if level == 0 and plane + ahead < planes:
                halos[plane + ahead] = assemble(plane + ahead)
        halos = following
        image = jnp.sum(jnp.where(image_row, total, 0.0), axis=1)
        part_ref[:, level] = image.reshape(groups, share, LANES)
        for step in range(1, members):
            other = lax.rem(me + step, members)
            copy = pltpu.make_async_remote_copy(
                src_ref=part_ref.at[other // shots_axis, level],
                dst_ref=gather_ref.at[me, level],
                send_sem=red_send.at[level, step],
                recv_sem=red_recv.at[level, step],
                device_id={"freq": other // shots_axis, "shot": lax.rem(other, shots_axis)},
                device_id_type=MESH,
            )
            copy.start()
            reductions.append(copy)
    gather_ref[me] = part_ref[freq]
    for copy in reductions:
        copy.wait()
    result = gather_ref[0]
    for index in range(1, members):
        result = result + gather_ref[index]
    for level in range(depth):
        out_ref[0, :, level, :] = result[level]


def body(records, source_pattern, wavelet, filters, vel_table, vel_index, freq_plan, counts):
    groups = lax.axis_size("freq")
    shots_axis = lax.axis_size("shot")
    shot_dev, rows, own_cols, samples = records.shape
    cols = source_pattern.shape[2]
    nref, _, taps, _, bin_total = filters.shape
    depth = vel_index.shape[0]
    planes = FPD
    lines = nref * 2 * taps
    members = groups * shots_axis
    scale = 1.0 / math.sqrt(planes * groups * shot_dev * shots_axis)
    dims = (groups, shots_axis, planes, rows, own_cols, taps, nref, depth, samples)
    strips = rows * own_cols // LANES
    packs = strips // 2 if strips % 2 == 0 else strips
    field_rows = (rows + 2 * (taps // 2)) * SUB
    share = rows // groups
    vmem = pl.BlockSpec(memory_space=pltpu.VMEM)
    anywhere = pl.BlockSpec(memory_space=pltpu.HBM)
    arguments = (
        records.reshape(shot_dev * rows * own_cols, samples),
        source_pattern,
        wavelet.T,
        filters.transpose(0, 2, 3, 1, 4).reshape(nref * taps, taps, 2, bin_total),
        vel_table,
        vel_index,
        freq_plan,
        counts,
    )
    arguments = tuple(pltpu.with_memory_space_constraint(a, pltpu.HBM) for a in arguments)
    scalars = (4, 6, 7)
    image = pl.pallas_call(
        functools.partial(kernel, dims),
        out_shape=jax.ShapeDtypeStruct((1, share, depth, cols), jnp.float32),
        in_specs=[anywhere] * len(arguments),
        out_specs=vmem,
        scratch_shapes=[
            (pltpu.SMEM if place in scalars else pltpu.VMEM)(array.shape, array.dtype)
            for place, array in enumerate(arguments)
        ] + [
            pltpu.VMEM((groups, planes, packs * SUB, LANES), jnp.bfloat16),
            pltpu.VMEM((groups, planes, packs * SUB, LANES), jnp.bfloat16),
            pltpu.VMEM((lines * SEG, bin_total), jnp.bfloat16),
            pltpu.VMEM((planes, taps * LANES, nref * 2 * LANES), jnp.bfloat16),
            pltpu.VMEM((rows * SUB, taps * LANES), jnp.bfloat16),
            pltpu.VMEM((planes, field_rows, LANES), jnp.float32),
            pltpu.VMEM((planes, field_rows, LANES), jnp.float32),
            pltpu.VMEM((groups, depth, share, LANES), jnp.float32),
            pltpu.VMEM((members, depth, share, LANES), jnp.float32),
            pltpu.SemaphoreType.DMA((len(arguments),)),
            pltpu.SemaphoreType.DMA((planes, groups)),
            pltpu.SemaphoreType.DMA((planes, groups)),
            pltpu.SemaphoreType.DMA((depth, planes)),
            pltpu.SemaphoreType.DMA((depth, planes)),
            pltpu.SemaphoreType.DMA((depth, members)),
            pltpu.SemaphoreType.DMA((depth, members)),
        ],
        compiler_params=pltpu.CompilerParams(
            collective_id=0, has_side_effects=True, vmem_limit_bytes=24 << 20
        ),
    )(*arguments)
    return image * scale


def solution(mesh):
    return jax.shard_map(
        body,
        mesh=mesh,
        in_specs=(
            P(("group", "shot"), "half", "freq", None),
            P(("group", "shot"), "half", None),
            P(),
            P(),
            P(),
            P("group", "half", None),
            P(),
            P(),
        ),
        out_specs=P("half", "freq", "group", None),
        check_vma=False,
    )
```

```python
import functools
import math

import jax
import jax.numpy as jnp
from jax import lax
from jax.experimental import pallas as pl
from jax.experimental.pallas import tpu as pltpu
from jax.sharding import PartitionSpec as P

LANES = 128
SUB = 8
SEG = 16
SLOT = 32
MESH = pl.DeviceIdType.MESH
FPD = 3


def kernel(
    dims,
    records_any, pattern_any, wavelet_any, filters_any, table_any, index_any, plan_any, counts_any,
    out_ref,
    records_ref, pattern_ref, wavelet_ref, filters_ref, table_ref, index_ref, plan_ref, counts_ref,
    send_ref, recv_ref, edge_ref, edges_ref, beside_ref, taps_ref, lines_ref, bands_ref, stack_ref, field0_ref, field1_ref,
    part_ref, gather_ref,
    load_sem, a2a_send, a2a_recv, edge_send, edge_recv, beside_send, beside_recv, halo_send, halo_recv, red_send, red_recv,
):
    groups, shots_axis, planes, rows, own_cols, taps, nref, depth, samples, packs, pairs, edge_packs, margin = dims
    half_taps = taps // 2
    pad = half_taps * SUB
    body_rows = rows * SUB
    slack = margin * SUB
    freq = lax.axis_index("freq")
    shot = lax.axis_index("shot")
    half = lax.axis_index("half")
    members = groups * shots_axis
    me = freq * shots_axis + shot

    barrier = pltpu.get_barrier_semaphore()
    for step in range(1, groups):
        other = lax.rem(freq + step, groups)
        pl.semaphore_signal(barrier, inc=1, device_id={"freq": other}, device_id_type=MESH)
        pl.semaphore_signal(barrier, inc=1, device_id={"freq": other, "half": 1 - half}, device_id_type=MESH)
    for step in range(1, shots_axis):
        other = lax.rem(shot + step, shots_axis)
        pl.semaphore_signal(barrier, inc=1, device_id={"shot": other}, device_id_type=MESH)
    pl.semaphore_signal(barrier, inc=1, device_id={"half": 1 - half}, device_id_type=MESH)

    loads = []
    for place, (source, target) in enumerate((
        (counts_any, counts_ref), (plan_any, plan_ref), (records_any, records_ref),
        (filters_any, filters_ref), (wavelet_any, wavelet_ref), (table_any, table_ref),
        (index_any, index_ref), (pattern_any, pattern_ref),
    )):
        copy = pltpu.make_async_copy(source, target, load_sem.at[place])
        copy.start()
        loads.append(copy)
    loads[0].wait()
    loads[1].wait()

    slots = plan_ref.shape[1]

    def bin_of(wanted):
        run = jnp.int32(0)
        start = jnp.int32(0)
        holder = jnp.int32(0)
        for group in range(groups):
            run = run + counts_ref[group]
            past = run <= wanted
            holder = holder + past.astype(jnp.int32)
            start = jnp.where(past, run, start)
        holder = jnp.minimum(holder, groups - 1)
        return plan_ref[holder, jnp.minimum(wanted - start, slots - 1)]

    per_group = SUB // 2
    wave_plane = lax.broadcasted_iota(jnp.int32, (SUB, samples), 0) // 2
    wave_part = lax.broadcasted_iota(jnp.int32, (SUB, samples), 0) % 2
    sample = lax.broadcasted_iota(jnp.int32, (SUB, samples), 1)
    waves = []
    for first in range(0, groups * planes, per_group):
        bins = jnp.zeros((SUB, samples), jnp.int32)
        for plane in range(per_group):
            bins = jnp.where(wave_plane == plane, bin_of(jnp.int32(first + plane)), bins)
        phase = (bins * sample + wave_part * (samples // 4)) & (samples - 1)
        waves.append(phase.astype(jnp.float32) * (2.0 * math.pi / samples))
    waves = jnp.concatenate(waves, axis=0) if len(waves) > 1 else waves[0]
    waves = (jnp.cos(waves) * (1.0 / math.sqrt(samples))).astype(jnp.bfloat16)
    table_rows = groups * planes * SUB
    spread_row = lax.broadcasted_iota(jnp.int32, (table_rows, waves.shape[0]), 0)
    spread_col = lax.broadcasted_iota(jnp.int32, (table_rows, waves.shape[0]), 1)
    spread_to = (spread_row // SUB) * 2 + (spread_row % SUB) // (SUB // 2)
    spread_hot = (spread_col == spread_to).astype(jnp.float32).astype(jnp.bfloat16)
    dft = jnp.dot(spread_hot, waves, preferred_element_type=jnp.float32).astype(jnp.bfloat16)

    sub_row = lax.broadcasted_iota(jnp.int32, (SUB, LANES), 0)
    odd_shot = (sub_row & 1) == 1
    second = (sub_row & 2) == 2
    upper = sub_row >= SUB // 2

    half_lanes = rows * own_cols
    loads[2].wait()
    spectra = []
    for index in range(2):
        block = records_ref[index * half_lanes:(index + 1) * half_lanes, :]
        spectra.append(
            lax.dot_general(dft, block, (((1,), (1,)), ((), ())), preferred_element_type=jnp.float32)
        )
    for holder in range(groups):
        for plane in range(planes):
            pieces = []
            base = (holder * planes + plane) * SUB
            for pack in range(packs):
                chosen = []
                for pair in range(pairs):
                    at = (pack * pairs + pair) * LANES
                    chosen.append(
                        jnp.where(
                            odd_shot,
                            spectra[1][base:base + SUB, at:at + LANES],
                            spectra[0][base:base + SUB, at:at + LANES],
                        )
                    )
                pieces.append(chosen[0] if pairs == 1 else jnp.where(second, chosen[1], chosen[0]))
            piece = jnp.concatenate(pieces, axis=0) if packs > 1 else pieces[0]
            send_ref[holder, plane] = piece.astype(jnp.bfloat16)
            border = jnp.where(half == 0, piece[(packs - edge_packs) * SUB:, :], piece[:edge_packs * SUB, :])
            edge_ref[holder, plane] = border.astype(jnp.bfloat16)
    recv_ref[freq] = send_ref[freq]

    pl.semaphore_wait(barrier, 2 * (groups - 1) + shots_axis)
    for copy in loads[3:]:
        copy.wait()

    exchanges = []
    for plane in range(planes):
        arriving = []
        for step in range(1, groups):
            other = lax.rem(freq + step, groups)
            copy = pltpu.make_async_remote_copy(
                src_ref=send_ref.at[other, plane],
                dst_ref=recv_ref.at[freq, plane],
                send_sem=a2a_send.at[plane, step],
                recv_sem=a2a_recv.at[plane, step],
                device_id={"freq": other},
                device_id_type=MESH,
            )
            copy.start()
            arriving.append(copy)
        for step in range(groups):
            other = lax.rem(freq + step, groups)
            copy = pltpu.make_async_remote_copy(
                src_ref=edge_ref.at[other, plane],
                dst_ref=edges_ref.at[freq, plane],
                send_sem=edge_send.at[plane, step],
                recv_sem=edge_recv.at[plane, step],
                device_id={"freq": other, "half": 1 - half},
                device_id_type=MESH,
            )
            copy.start()
            arriving.append(copy)
        exchanges.append(arriving)
    beside = pltpu.make_async_remote_copy(
        src_ref=pattern_ref,
        dst_ref=beside_ref,
        send_sem=beside_send.at[0],
        recv_sem=beside_recv.at[0],
        device_id={"half": 1 - half},
        device_id_type=MESH,
    )
    beside.start()

    bin_total = taps_ref.shape[1]
    own_bins = [bin_of(freq * planes + plane) for plane in range(planes)]
    segments = nref * taps
    taps_ref[...] = jnp.zeros_like(taps_ref)
    for segment in range(segments):
        for tap in range(taps):
            at = segment * 2 * SEG + 2 * tap
            taps_ref[at:at + 2, :] = filters_ref[segment, tap]
    bin_lane = lax.broadcasted_iota(jnp.int32, (planes * SUB, bin_total), 1)
    bin_row = lax.broadcasted_iota(jnp.int32, (planes * SUB, bin_total), 0) // SUB
    wanted_bin = jnp.full((planes * SUB, bin_total), -1, jnp.int32)
    for plane in range(planes):
        wanted_bin = jnp.where(bin_row == plane, own_bins[plane], wanted_bin)
    bin_hot = (wanted_bin == bin_lane).astype(jnp.float32).astype(jnp.bfloat16)
    picked = lax.dot_general(
        bin_hot, taps_ref[...], (((1,), (1,)), ((), ())), preferred_element_type=jnp.float32
    ).astype(jnp.bfloat16)
    per_tile = LANES // SLOT
    pick_lane = lax.broadcasted_iota(jnp.int32, (LANES, 2 * LANES), 0)
    turn_lane = lax.broadcasted_iota(jnp.int32, (LANES, 2 * LANES), 1)
    turn = (
        (pick_lane // (2 * SEG) == turn_lane // (2 * SLOT))
        & (pick_lane % 2 == (turn_lane // SLOT) % 2)
        & ((pick_lane % (2 * SEG)) // 2 + turn_lane % SLOT == taps - 1)
    ).astype(jnp.float32).astype(jnp.bfloat16)
    for at in range(0, segments * 2 * SEG, LANES):
        width = min(LANES, segments * 2 * SEG - at)
        turned = jnp.dot(picked[:, at:at + width], turn[:width, :], preferred_element_type=jnp.float32)
        first = at // SEG
        for line in range(first, min(first + 2 * per_tile, 2 * segments), 2):
            place = (line - first) * SLOT
            for plane in range(planes):
                base = turned[plane * SUB:(plane + 1) * SUB, place // LANES * LANES:place // LANES * LANES + LANES]
                shift = -(place % LANES) % LANES
                own = pltpu.roll(base, shift, 1, stride=1, stride_axis=0)
                after = pltpu.roll(base, (shift - SLOT) % LANES, 1, stride=1, stride_axis=0)
                lines_ref[plane, line * SUB:(line + 2) * SUB, :] = jnp.concatenate([own, after], axis=0).astype(jnp.bfloat16)
    spread = lax.broadcasted_iota(jnp.int32, (SLOT, LANES), 1) - lax.broadcasted_iota(jnp.int32, (SLOT, LANES), 0)
    rest = jnp.zeros((LANES - SLOT, 2 * LANES), jnp.bfloat16)
    placed = lines_ref[...].reshape(planes * 2 * segments * SUB, LANES)
    for first in range(0, LANES, 2 * SUB):
        moves = jnp.concatenate(
            [(spread == first + more - half_taps).astype(jnp.float32) for more in (0, SUB)], axis=1
        ).astype(jnp.bfloat16)
        block = jnp.dot(placed, jnp.concatenate([moves, rest], axis=0), preferred_element_type=jnp.float32)
        for plane in range(planes):
            for line in range(2 * segments):
                segment = line // 2
                at = (segment % taps) * LANES + first
                side = (segment // taps) * 2 + line % 2
                start = (plane * 2 * segments + line) * SUB
                bands_ref[plane, at:at + 2 * SUB, side * LANES:(side + 1) * LANES] = jnp.concatenate(
                    [block[start:start + SUB, :LANES], block[start:start + SUB, LANES:]], axis=0
                ).astype(jnp.bfloat16)

    blends = []
    for level in range(depth):
        classes = index_ref[level]
        weight = jnp.zeros(classes.shape, jnp.float32)
        for entry in range(table_ref.shape[0]):
            weight = jnp.where(classes == entry, table_ref[entry], weight)
        blends.append(weight)

    outer = pl.multiple_of(half * (body_rows + pad), SUB)
    outer0 = pl.multiple_of(slack + half * (body_rows + pad), SUB)
    for plane in range(planes):
        field0_ref[plane, pl.ds(outer0, pad), :] = jnp.zeros((pad, LANES), jnp.float32)
        field1_ref[plane, pl.ds(outer, pad), :] = jnp.zeros((pad, LANES), jnp.float32)
    pattern = [pattern_ref[index].astype(jnp.float32) for index in range(2)]
    wave_lane = lax.broadcasted_iota(jnp.int32, wavelet_ref.shape, 1)
    gains = []
    for plane in range(planes):
        gain = jnp.sum(
            jnp.where(wave_lane == own_bins[plane], wavelet_ref[...], 0.0), axis=1, keepdims=True
        )
        gains.append(
            jnp.where(
                upper,
                jnp.broadcast_to(gain[1:2, :], (SUB, LANES)),
                jnp.broadcast_to(gain[0:1, :], (SUB, LANES)),
            )
        )

    inner = pl.multiple_of(body_rows - half * (body_rows - pad), SUB)
    target = pl.multiple_of(half * (body_rows + pad), SUB)

    def swap(level, plane):
        field_ref = field1_ref
        copy = pltpu.make_async_remote_copy(
            src_ref=field_ref.at[plane, pl.ds(inner, pad), :],
            dst_ref=field_ref.at[plane, pl.ds(target, pad), :],
            send_sem=halo_send.at[level - 1, plane],
            recv_sem=halo_recv.at[level - 1, plane],
            device_id={"half": 1 - half},
            device_id_type=MESH,
        )
        copy.start()
        return copy

    strip_rows = LANES // own_cols
    edge_rows = edge_packs * pairs * strip_rows
    edge_at = pl.multiple_of(
        jnp.where(half == 0, slack + pad + body_rows, slack + pad - edge_rows * SUB), SUB
    )
    beside.wait()
    besides = []
    for index in range(2):
        other_half = beside_ref[index].astype(jnp.float32)
        besides.append(jnp.where(half == 0, other_half[:edge_rows, :], other_half[rows - edge_rows:, :]))

    def unfold(blocks, count, patterns, plane, put):
        lane = lax.broadcasted_iota(jnp.int32, (count * SUB, LANES), 1) // own_cols
        for low in range(strip_rows):
            merged = jnp.zeros((count * SUB, LANES), jnp.float32)
            for group in range(groups):
                shift = ((group - low) * own_cols) % LANES
                moved = blocks[group] if shift == 0 else pltpu.roll(blocks[group], shift, 1)
                merged = jnp.where(lane == group, moved, merged)
            for pack in range(count):
                value = merged[pack * SUB:(pack + 1) * SUB, :]
                for pair in range(pairs):
                    row = (pack * pairs + pair) * strip_rows + low
                    receiver = value
                    if pairs == 2 and pair == 0:
                        receiver = pltpu.roll(value, 2, 0)
                    source = jnp.where(
                        odd_shot, patterns[1][row:row + 1, :], patterns[0][row:row + 1, :]
                    ) * gains[plane]
                    source = source.astype(jnp.bfloat16).astype(jnp.float32)
                    put(row, jnp.where(second, receiver, source))

    def assemble(plane):
        for copy in exchanges[plane]:
            copy.wait()

        def put_body(row, value):
            at = slack + pad + row * SUB
            field0_ref[plane, at:at + SUB, :] = value

        def put_edge(row, value):
            field0_ref[plane, pl.ds(pl.multiple_of(edge_at + row * SUB, SUB), SUB), :] = value

        unfold([recv_ref[group, plane].astype(jnp.float32) for group in range(groups)], packs, pattern, plane, put_body)
        unfold([edges_ref[group, plane].astype(jnp.float32) for group in range(groups)], edge_packs, besides, plane, put_edge)

    row3 = lax.broadcasted_iota(jnp.int32, (rows, SUB, LANES), 1)
    sign = jnp.where(row3 >= SUB // 2, 1.0, -1.0)
    image_row = (row3 & 2) == 0
    share = rows // groups

    def extrapolate(level, plane):
        field_ref, start = (field0_ref, slack) if level == 0 else (field1_ref, 0)
        for tap_row in range(taps):
            at = start + tap_row * SUB
            stack_ref[:, tap_row * LANES:(tap_row + 1) * LANES] = field_ref[
                plane, at:at + body_rows, :
            ].astype(jnp.bfloat16)
        sides = []
        for side in range(nref):
            both = jnp.dot(
                stack_ref[...],
                bands_ref[plane, :, 2 * side * LANES:2 * (side + 1) * LANES],
                preferred_element_type=jnp.float32,
            )
            direct = both[:, :LANES].reshape(rows, SUB, LANES)
            crossed = both[:, LANES:].reshape(rows, SUB, LANES)
            sides.append(direct + sign * pltpu.roll(crossed, SUB // 2, 1))
        value = sides[0] + blends[level][:, None, :] * (sides[1] - sides[0])
        value = value.astype(jnp.bfloat16).astype(jnp.float32)
        copy = None
        if level + 1 < depth:
            field1_ref[plane, pad:pad + body_rows, :] = value.reshape(body_rows, LANES)
            copy = swap(level + 1, plane)
        return value * pltpu.roll(value, SUB - 2, 1), copy

    halos = {}
    reductions = []
    for level in range(depth):
        total = jnp.zeros((rows, SUB, LANES), jnp.float32)
        following = {}
        for plane in range(planes):
            if level == 0:
                assemble(plane)
            else:
                halos[plane].wait()
            term, following[plane] = extrapolate(level, plane)
            total = total + term
        halos = following
        image = jnp.sum(jnp.where(image_row, total, 0.0), axis=1)
        part_ref[:, level] = image.reshape(groups, share, LANES)
        for step in range(1, members):
            other = lax.rem(me + step, members)
            copy = pltpu.make_async_remote_copy(
                src_ref=part_ref.at[other // shots_axis, level],
                dst_ref=gather_ref.at[me, level],
                send_sem=red_send.at[level, step],
                recv_sem=red_recv.at[level, step],
                device_id={"freq": other // shots_axis, "shot": lax.rem(other, shots_axis)},
                device_id_type=MESH,
            )
            copy.start()
            reductions.append(copy)
    gather_ref[me] = part_ref[freq]
    for copy in reductions:
        copy.wait()
    result = gather_ref[0]
    for index in range(1, members):
        result = result + gather_ref[index]
    for level in range(depth):
        out_ref[0, :, level, :] = result[level]


def body(records, source_pattern, wavelet, filters, vel_table, vel_index, freq_plan, counts):
    groups = lax.axis_size("freq")
    shots_axis = lax.axis_size("shot")
    shot_dev, rows, own_cols, samples = records.shape
    cols = source_pattern.shape[2]
    nref, _, taps, _, bin_total = filters.shape
    depth = vel_index.shape[0]
    planes = FPD
    lines = nref * 2 * taps
    members = groups * shots_axis
    scale = 1.0 / math.sqrt(planes * groups * shot_dev * shots_axis)
    strips = rows * own_cols // LANES
    pairs = 2 if strips % 2 == 0 else 1
    packs = strips // pairs
    pack_rows = pairs * (LANES // own_cols)
    edge_packs = min(packs, -(-(taps // 2) // pack_rows))
    margin = edge_packs * pack_rows - taps // 2
    dims = (groups, shots_axis, planes, rows, own_cols, taps, nref, depth, samples, packs, pairs, edge_packs, margin)
    field_rows = (rows + 2 * (taps // 2)) * SUB
    share = rows // groups
    vmem = pl.BlockSpec(memory_space=pltpu.VMEM)
    anywhere = pl.BlockSpec(memory_space=pltpu.HBM)
    arguments = (
        records.reshape(shot_dev * rows * own_cols, samples),
        source_pattern,
        wavelet.T,
        filters.transpose(0, 2, 3, 1, 4).reshape(nref * taps, taps, 2, bin_total),
        vel_table,
        vel_index,
        freq_plan,
        counts,
    )
    arguments = tuple(pltpu.with_memory_space_constraint(a, pltpu.HBM) for a in arguments)
    scalars = (4, 6, 7)
    image = pl.pallas_call(
        functools.partial(kernel, dims),
        out_shape=jax.ShapeDtypeStruct((1, share, depth, cols), jnp.float32),
        in_specs=[anywhere] * len(arguments),
        out_specs=vmem,
        scratch_shapes=[
            (pltpu.SMEM if place in scalars else pltpu.VMEM)(array.shape, array.dtype)
            for place, array in enumerate(arguments)
        ] + [
            pltpu.VMEM((groups, planes, packs * SUB, LANES), jnp.bfloat16),
            pltpu.VMEM((groups, planes, packs * SUB, LANES), jnp.bfloat16),
            pltpu.VMEM((groups, planes, edge_packs * SUB, LANES), jnp.bfloat16),
            pltpu.VMEM((groups, planes, edge_packs * SUB, LANES), jnp.bfloat16),
            pltpu.VMEM(source_pattern.shape, source_pattern.dtype),
            pltpu.VMEM((lines * SEG, bin_total), jnp.bfloat16),
            pltpu.VMEM((planes, lines * SUB, LANES), jnp.bfloat16),
            pltpu.VMEM((planes, taps * LANES, nref * 2 * LANES), jnp.bfloat16),
            pltpu.VMEM((rows * SUB, taps * LANES), jnp.bfloat16),
            pltpu.VMEM((planes, field_rows + 2 * margin * SUB, LANES), jnp.float32),
            pltpu.VMEM((planes, field_rows, LANES), jnp.float32),
            pltpu.VMEM((groups, depth, share, LANES), jnp.float32),
            pltpu.VMEM((members, depth, share, LANES), jnp.float32),
            pltpu.SemaphoreType.DMA((len(arguments),)),
            pltpu.SemaphoreType.DMA((planes, groups)),
            pltpu.SemaphoreType.DMA((planes, groups)),
            pltpu.SemaphoreType.DMA((planes, groups)),
            pltpu.SemaphoreType.DMA((planes, groups)),
            pltpu.SemaphoreType.DMA((1,)),
            pltpu.SemaphoreType.DMA((1,)),
            pltpu.SemaphoreType.DMA((depth - 1, planes)),
            pltpu.SemaphoreType.DMA((depth - 1, planes)),
            pltpu.SemaphoreType.DMA((depth, members)),
            pltpu.SemaphoreType.DMA((depth, members)),
        ],
        compiler_params=pltpu.CompilerParams(
            collective_id=0, has_side_effects=True, vmem_limit_bytes=24 << 20
        ),
    )(*arguments)
    return image * scale


def solution(mesh):
    return jax.shard_map(
        body,
        mesh=mesh,
        in_specs=(
            P(("group", "shot"), "half", "freq", None),
            P(("group", "shot"), "half", None),
            P(),
            P(),
            P(),
            P("group", "half", None),
            P(),
            P(),
        ),
        out_specs=P("half", "freq", "group", None),
        check_vma=False,
    )
```

```python
import functools
import math

import jax
import jax.numpy as jnp
from jax import lax
from jax.experimental import pallas as pl
from jax.experimental.pallas import tpu as pltpu
from jax.sharding import PartitionSpec as P

LANES = 128
SUB = 8
SEG = 16
SLOT = 32
CHUNKS = 2
MESH = pl.DeviceIdType.MESH
FPD = 3


def kernel(
    dims,
    records_any, pattern_any, wavelet_any, filters_any, table_any, index_any, plan_any, counts_any,
    out_ref,
    records_ref, pattern_ref, wavelet_ref, filters_ref, table_ref, index_ref, plan_ref, counts_ref,
    send_ref, recv_ref, edge_ref, edges_ref, beside_ref, taps_ref, bands_ref, field0_ref, field1_ref,
    image_ref, part_ref, gather_ref,
    load_sem, a2a_send, a2a_recv, edge_send, edge_recv, beside_send, beside_recv, halo_send, halo_recv, red_send, red_recv,
):
    groups, shots_axis, planes, rows, own_cols, taps, nref, depth, samples, packs, pairs, edge_packs, margin = dims
    half_taps = taps // 2
    pad = half_taps // 2
    body_rows = rows // 2
    slack = margin // 2
    blocks_out = LANES // SLOT
    window = LANES // 2
    steps = (taps + 1) // 2
    freq = lax.axis_index("freq")
    shot = lax.axis_index("shot")
    half = lax.axis_index("half")
    members = groups * shots_axis
    me = freq * shots_axis + shot

    barrier = pltpu.get_barrier_semaphore()
    for step in range(1, groups):
        other = lax.rem(freq + step, groups)
        pl.semaphore_signal(barrier, inc=1, device_id={"freq": other}, device_id_type=MESH)
        pl.semaphore_signal(barrier, inc=1, device_id={"freq": other, "half": 1 - half}, device_id_type=MESH)
    for step in range(1, shots_axis):
        other = lax.rem(shot + step, shots_axis)
        pl.semaphore_signal(barrier, inc=1, device_id={"shot": other}, device_id_type=MESH)
    pl.semaphore_signal(barrier, inc=1, device_id={"half": 1 - half}, device_id_type=MESH)

    loads = []
    for place, (source, target) in enumerate((
        (counts_any, counts_ref), (plan_any, plan_ref), (records_any, records_ref),
        (filters_any, filters_ref), (wavelet_any, wavelet_ref), (table_any, table_ref),
        (index_any, index_ref), (pattern_any, pattern_ref),
    )):
        copy = pltpu.make_async_copy(source, target, load_sem.at[place])
        copy.start()
        loads.append(copy)
    loads[0].wait()
    loads[1].wait()

    slots = plan_ref.shape[1]

    def bin_of(wanted):
        run = jnp.int32(0)
        start = jnp.int32(0)
        holder = jnp.int32(0)
        for group in range(groups):
            run = run + counts_ref[group]
            past = run <= wanted
            holder = holder + past.astype(jnp.int32)
            start = jnp.where(past, run, start)
        holder = jnp.minimum(holder, groups - 1)
        return plan_ref[holder, jnp.minimum(wanted - start, slots - 1)]

    per_group = SUB // 2
    wave_plane = lax.broadcasted_iota(jnp.int32, (SUB, samples), 0) // 2
    wave_part = lax.broadcasted_iota(jnp.int32, (SUB, samples), 0) % 2
    sample = lax.broadcasted_iota(jnp.int32, (SUB, samples), 1)
    waves = []
    for first in range(0, groups * planes, per_group):
        bins = jnp.zeros((SUB, samples), jnp.int32)
        for plane in range(per_group):
            bins = jnp.where(wave_plane == plane, bin_of(jnp.int32(first + plane)), bins)
        phase = (bins * sample + wave_part * (samples // 4)) & (samples - 1)
        waves.append(phase.astype(jnp.float32) * (2.0 * math.pi / samples))
    waves = jnp.concatenate(waves, axis=0) if len(waves) > 1 else waves[0]
    waves = (jnp.cos(waves) * (1.0 / math.sqrt(samples))).astype(jnp.bfloat16)
    table_rows = groups * planes * SUB
    spread_row = lax.broadcasted_iota(jnp.int32, (table_rows, waves.shape[0]), 0)
    spread_col = lax.broadcasted_iota(jnp.int32, (table_rows, waves.shape[0]), 1)
    spread_to = (spread_row // SUB) * 2 + (spread_row % SUB) // (SUB // 2)
    spread_hot = (spread_col == spread_to).astype(jnp.float32).astype(jnp.bfloat16)
    dft = jnp.dot(spread_hot, waves, preferred_element_type=jnp.float32).astype(jnp.bfloat16)

    sub_row = lax.broadcasted_iota(jnp.int32, (SUB, LANES), 0)
    odd_shot = (sub_row & 1) == 1
    second = (sub_row & 2) == 2
    upper = sub_row >= SUB // 2

    half_lanes = rows * own_cols
    loads[2].wait()
    spectra = []
    for index in range(2):
        block = records_ref[index * half_lanes:(index + 1) * half_lanes, :]
        spectra.append(
            lax.dot_general(dft, block, (((1,), (1,)), ((), ())), preferred_element_type=jnp.float32)
        )
    for holder in range(groups):
        for plane in range(planes):
            pieces = []
            base = (holder * planes + plane) * SUB
            for pack in range(packs):
                chosen = []
                for pair in range(pairs):
                    at = (pack * pairs + pair) * LANES
                    chosen.append(
                        jnp.where(
                            odd_shot,
                            spectra[1][base:base + SUB, at:at + LANES],
                            spectra[0][base:base + SUB, at:at + LANES],
                        )
                    )
                pieces.append(chosen[0] if pairs == 1 else jnp.where(second, chosen[1], chosen[0]))
            piece = jnp.concatenate(pieces, axis=0) if packs > 1 else pieces[0]
            send_ref[holder, plane] = piece.astype(jnp.bfloat16)
            border = jnp.where(half == 0, piece[(packs - edge_packs) * SUB:, :], piece[:edge_packs * SUB, :])
            edge_ref[holder, plane] = border.astype(jnp.bfloat16)
    recv_ref[freq] = send_ref[freq]

    pl.semaphore_wait(barrier, 2 * (groups - 1) + shots_axis)
    for copy in loads[3:]:
        copy.wait()

    def drain(ref, sem):
        pltpu.make_async_copy(ref, ref, sem).wait()

    for plane in range(planes):
        for step in range(1, groups):
            other = lax.rem(freq + step, groups)
            copy = pltpu.make_async_remote_copy(
                src_ref=send_ref.at[other, plane],
                dst_ref=recv_ref.at[freq, plane],
                send_sem=a2a_send.at[0],
                recv_sem=a2a_recv.at[plane],
                device_id={"freq": other},
                device_id_type=MESH,
            )
            copy.start()
        for step in range(groups):
            other = lax.rem(freq + step, groups)
            copy = pltpu.make_async_remote_copy(
                src_ref=edge_ref.at[other, plane],
                dst_ref=edges_ref.at[freq, plane],
                send_sem=edge_send.at[0],
                recv_sem=edge_recv.at[plane],
                device_id={"freq": other, "half": 1 - half},
                device_id_type=MESH,
            )
            copy.start()
    beside = pltpu.make_async_remote_copy(
        src_ref=pattern_ref,
        dst_ref=beside_ref,
        send_sem=beside_send.at[0],
        recv_sem=beside_recv.at[0],
        device_id={"half": 1 - half},
        device_id_type=MESH,
    )
    beside.start()

    bin_total = taps_ref.shape[1]
    own_bins = [bin_of(freq * planes + plane) for plane in range(planes)]
    segments = nref * taps
    taps_ref[...] = jnp.zeros_like(taps_ref)
    for segment in range(segments):
        for tap in range(taps):
            at = ((segment % taps) * nref + segment // taps) * 2 * SEG + 2 * tap
            taps_ref[at:at + 2, :] = filters_ref[segment, tap]
    bin_lane = lax.broadcasted_iota(jnp.int32, (planes * SUB, bin_total), 1)
    bin_row = lax.broadcasted_iota(jnp.int32, (planes * SUB, bin_total), 0) // SUB
    wanted_bin = jnp.full((planes * SUB, bin_total), -1, jnp.int32)
    for plane in range(planes):
        wanted_bin = jnp.where(bin_row == plane, own_bins[plane], wanted_bin)
    bin_hot = (wanted_bin == bin_lane).astype(jnp.float32).astype(jnp.bfloat16)
    picked = lax.dot_general(
        bin_hot, taps_ref[...], (((1,), (1,)), ((), ())), preferred_element_type=jnp.float32
    ).astype(jnp.bfloat16)
    per_tile = LANES // SLOT
    pick_lane = lax.broadcasted_iota(jnp.int32, (LANES, 2 * LANES), 0)
    turn_lane = lax.broadcasted_iota(jnp.int32, (LANES, 2 * LANES), 1)
    turn = (
        (pick_lane // (2 * SEG) == turn_lane // (2 * SLOT))
        & (pick_lane % 2 == (turn_lane // SLOT) % 2)
        & ((pick_lane % (2 * SEG)) // 2 + turn_lane % SLOT == taps - 1)
    ).astype(jnp.float32).astype(jnp.bfloat16)
    bases = [[] for _ in range(planes)]
    per_row = nref * 2 * SEG
    for at in range(0, segments * 2 * SEG, LANES):
        width = min(LANES, segments * 2 * SEG - at)
        turned = jnp.dot(picked[:, at:at + width], turn[:width, :], preferred_element_type=jnp.float32)
        for more in range(width // per_row):
            for plane in range(planes):
                base = turned[plane * SUB:(plane + 1) * SUB, more * LANES:(more + 1) * LANES]
                bases[plane].append(pltpu.roll(base, 0, 1, stride=1, stride_axis=0))
    placed = jnp.concatenate(sum(bases, []), axis=0).astype(jnp.bfloat16)
    lane_in = lax.broadcasted_iota(jnp.int32, (LANES, LANES), 0)
    lane_out = lax.broadcasted_iota(jnp.int32, (LANES, LANES), 1)
    spread = jnp.where(lane_in // SLOT == lane_out // SLOT, lane_out - lane_in, 2 * LANES)
    bands_ref[...] = jnp.zeros_like(bands_ref)
    for first in range(0, SLOT + taps - 1, 2 * SUB):
        moves = jnp.concatenate(
            [(spread == first + more - taps + 1).astype(jnp.float32) for more in (0, SUB)], axis=1
        ).astype(jnp.bfloat16)
        block = jnp.dot(placed, moves, preferred_element_type=jnp.float32)
        for plane in range(planes):
            for tap_row in range(taps):
                start = (plane * taps + tap_row) * SUB
                piece = jnp.concatenate(
                    [block[start:start + SUB, :LANES], block[start:start + SUB, LANES:]], axis=0
                ).astype(jnp.bfloat16)
                for odd in range(2):
                    at = (tap_row + odd) * window + first
                    bands_ref[plane, at:at + 2 * SUB, odd * LANES:(odd + 1) * LANES] = piece

    slot = lax.broadcasted_iota(jnp.int32, (body_rows, LANES), 1) // SLOT
    blends = []
    for level in range(depth):
        by_parity = []
        for odd in range(2):
            classes = index_ref[level, pl.ds(odd, body_rows, stride=2), :]
            weight = jnp.zeros(classes.shape, jnp.float32)
            for entry in range(table_ref.shape[0]):
                weight = jnp.where(classes == entry, table_ref[entry], weight)
            wide = []
            for place in range(blocks_out):
                own = jnp.where(slot == place, weight, 0.0)
                own = own + pltpu.roll(own, SLOT, 1)
                own = own + pltpu.roll(own, window, 1)
                wide.append(jnp.where(slot < 2, 1.0 - own, own))
            by_parity.append(wide)
        blends.append(by_parity)

    outer = half * (body_rows + pad)
    for plane in range(planes):
        blank = jnp.zeros((pad, blocks_out * SUB, LANES), jnp.bfloat16)
        field0_ref[plane, pl.ds(slack + outer, pad)] = blank
        field1_ref[plane, pl.ds(outer, pad)] = blank
    pattern = [pattern_ref[index].astype(jnp.float32) for index in range(2)]
    wave_lane = lax.broadcasted_iota(jnp.int32, wavelet_ref.shape, 1)
    gains = []
    for plane in range(planes):
        gain = jnp.sum(
            jnp.where(wave_lane == own_bins[plane], wavelet_ref[...], 0.0), axis=1, keepdims=True
        )
        gains.append(
            jnp.where(
                upper,
                jnp.broadcast_to(gain[1:2, :], (SUB, LANES)),
                jnp.broadcast_to(gain[0:1, :], (SUB, LANES)),
            )
        )

    inner = body_rows - half * (body_rows - pad)
    target = half * (body_rows + pad)

    def swap(level, plane):
        field_ref = field1_ref
        copy = pltpu.make_async_remote_copy(
            src_ref=field_ref.at[plane, pl.ds(inner, pad)],
            dst_ref=field_ref.at[plane, pl.ds(target, pad)],
            send_sem=halo_send.at[level - 1, plane],
            recv_sem=halo_recv.at[level - 1, plane],
            device_id={"half": 1 - half},
            device_id_type=MESH,
        )
        copy.start()
        return copy

    strip_rows = LANES // own_cols
    edge_rows = edge_packs * pairs * strip_rows
    edge_at = jnp.where(half == 0, slack + pad + body_rows, slack + pad - edge_rows // 2)
    beside.wait()
    besides = []
    for index in range(2):
        other_half = beside_ref[index].astype(jnp.float32)
        besides.append(jnp.where(half == 0, other_half[:edge_rows, :], other_half[rows - edge_rows:, :]))

    def windows(even, odd):
        lane3 = lax.broadcasted_iota(jnp.int32, even.shape, 2)
        side = lane3 % window
        turned = []
        for place in range(blocks_out):
            start = place * SLOT - half_taps
            seen = jnp.where(
                lane3 < window,
                pltpu.roll(even, -start % LANES, 2),
                pltpu.roll(odd, (window - start) % LANES, 2),
            )
            if start < 0:
                seen = jnp.where(side < -start, 0.0, seen)
            if start + SLOT + taps - 1 > LANES:
                seen = jnp.where(side >= LANES - start, 0.0, seen)
            turned.append(seen)
        return jnp.concatenate(turned, axis=1).astype(jnp.bfloat16)

    def unfold(blocks, count, patterns, plane):
        found = {}
        lane = lax.broadcasted_iota(jnp.int32, (count * SUB, LANES), 1) // own_cols
        for low in range(strip_rows):
            merged = jnp.zeros((count * SUB, LANES), jnp.float32)
            for group in range(groups):
                shift = ((group - low) * own_cols) % LANES
                moved = blocks[group] if shift == 0 else pltpu.roll(blocks[group], shift, 1)
                merged = jnp.where(lane == group, moved, merged)
            for pack in range(count):
                value = merged[pack * SUB:(pack + 1) * SUB, :]
                for pair in range(pairs):
                    row = (pack * pairs + pair) * strip_rows + low
                    receiver = value
                    if pairs == 2 and pair == 0:
                        receiver = pltpu.roll(value, 2, 0)
                    source = jnp.where(
                        odd_shot, patterns[1][row:row + 1, :], patterns[0][row:row + 1, :]
                    ) * gains[plane]
                    source = source.astype(jnp.bfloat16).astype(jnp.float32)
                    found[row] = jnp.where(second, receiver, source)
        return windows(
            jnp.stack([found[row] for row in range(0, len(found), 2)]),
            jnp.stack([found[row] for row in range(1, len(found), 2)]),
        )

    def arrive(plane):
        drain(recv_ref.at[pl.ds(0, groups - 1), plane], a2a_recv.at[plane])
        drain(edges_ref.at[:, plane], edge_recv.at[plane])

    def assemble(plane):
        blocks = [recv_ref[group, plane].astype(jnp.float32) for group in range(groups)]
        edges = [edges_ref[group, plane].astype(jnp.float32) for group in range(groups)]
        field0_ref[plane, slack + pad:slack + pad + body_rows] = unfold(blocks, packs, pattern, plane)
        field0_ref[plane, pl.ds(edge_at, edge_rows // 2)] = unfold(edges, edge_packs, besides, plane)

    part_shape = (body_rows // CHUNKS, SUB, LANES)
    row3 = lax.broadcasted_iota(jnp.int32, (body_rows, SUB, LANES), 1)
    slot3 = lax.broadcasted_iota(jnp.int32, part_shape, 2) // SLOT
    low3 = slot3 < 2
    middle3 = (slot3 == 1) | (slot3 == 2)
    even3 = slot3 % 2 == 0
    sign = jnp.where(lax.broadcasted_iota(jnp.int32, part_shape, 1) >= SUB // 2, 1.0, -1.0)
    image_row = (row3 & 2) == 0
    share = rows // groups

    def cross(value):
        return sign * pltpu.roll(value, SUB // 2, 1)

    def multiply(level, plane):
        field_ref, start = (field0_ref, slack) if level == 0 else (field1_ref, 0)
        chunk = body_rows // CHUNKS
        products = []
        for at in range(start, start + body_rows, chunk):
            seen = jnp.concatenate(
                [
                    field_ref[plane, at + step:at + step + chunk].reshape(chunk * blocks_out * SUB, LANES)
                    for step in range(steps)
                ],
                axis=1,
            )
            products.append(jnp.dot(seen, bands_ref[plane], preferred_element_type=jnp.float32))
        return products

    def finish(level, plane, products):
        chunk = body_rows // CHUNKS
        parts = [[], []]
        for index, both in enumerate(products):
            both = both.reshape(chunk, blocks_out, SUB, 2 * LANES)
            for odd in range(2):
                z = [
                    both[:, place, :, odd * LANES:(odd + 1) * LANES]
                    * blends[level][odd][place][index * chunk:(index + 1) * chunk][:, None, :]
                    for place in range(blocks_out)
                ]
                first = jnp.where(low3, z[0], z[2]) + pltpu.roll(jnp.where(low3, z[2], z[0]), window, 2)
                after = jnp.where(middle3, z[1], z[3]) + pltpu.roll(jnp.where(middle3, z[3], z[1]), window, 2)
                value = jnp.where(even3, first, cross(after)) + pltpu.roll(
                    jnp.where(even3, after, cross(first)), LANES - SLOT, 2
                )
                parts[odd].append(value.astype(jnp.bfloat16).astype(jnp.float32))
        values = [jnp.concatenate(part, axis=0) for part in parts]
        copy = None
        if level + 1 < depth:
            field1_ref[plane, pad:pad + body_rows] = windows(*values)
            copy = swap(level + 1, plane)
        return [value * pltpu.roll(value, SUB - 2, 1) for value in values], copy

    halos = {}
    totals = {}

    def settle(level, plane, products):
        terms, halos[level + 1, plane] = finish(level, plane, products)
        if plane:
            terms = [total + term for total, term in zip(totals[level], terms)]
        totals[level] = terms
        if plane + 1 == planes:
            reduce(level)

    def reduce(level):
        for odd in range(2):
            image_ref[pl.ds(odd, body_rows, stride=2), :] = jnp.sum(
                jnp.where(image_row, totals[level][odd], 0.0), axis=1
            )
        image = image_ref[...]
        part_ref[:, level] = image.reshape(groups, share, LANES)
        for step in range(1, members):
            other = lax.rem(me + step, members)
            copy = pltpu.make_async_remote_copy(
                src_ref=part_ref.at[other // shots_axis, level],
                dst_ref=gather_ref.at[me, level],
                send_sem=red_send.at[0],
                recv_sem=red_recv.at[0],
                device_id={"freq": other // shots_axis, "shot": lax.rem(other, shots_axis)},
                device_id_type=MESH,
            )
            copy.start()
    arrive(0)
    assemble(0)
    for plane in range(1, planes):
        arrive(plane)
    waiting = None
    for level in range(depth):
        for plane in range(planes):
            if level:
                halos[level, plane].wait()
            elif plane:
                assemble(plane)
            products = multiply(level, plane)
            if waiting is not None:
                settle(*waiting)
            waiting = (level, plane, products)
    settle(*waiting)
    gather_ref[me] = part_ref[freq]
    drain(gather_ref.at[pl.ds(0, members - 1)], red_recv.at[0])
    drain(gather_ref.at[pl.ds(0, members - 1)], red_send.at[0])
    drain(send_ref.at[pl.ds(0, groups - 1)], a2a_send.at[0])
    drain(edge_ref, edge_send.at[0])
    result = gather_ref[0]
    for index in range(1, members):
        result = result + gather_ref[index]
    for level in range(depth):
        out_ref[0, :, level, :] = result[level]


def body(records, source_pattern, wavelet, filters, vel_table, vel_index, freq_plan, counts):
    groups = lax.axis_size("freq")
    shots_axis = lax.axis_size("shot")
    shot_dev, rows, own_cols, samples = records.shape
    cols = source_pattern.shape[2]
    nref, _, taps, _, bin_total = filters.shape
    depth = vel_index.shape[0]
    planes = FPD
    lines = nref * 2 * taps
    members = groups * shots_axis
    scale = 1.0 / math.sqrt(planes * groups * shot_dev * shots_axis)
    strips = rows * own_cols // LANES
    pairs = 2 if strips % 2 == 0 else 1
    packs = strips // pairs
    pack_rows = pairs * (LANES // own_cols)
    edge_packs = min(packs, -(-(taps // 2) // pack_rows))
    margin = edge_packs * pack_rows - taps // 2
    dims = (groups, shots_axis, planes, rows, own_cols, taps, nref, depth, samples, packs, pairs, edge_packs, margin)
    row_pairs = rows // 2 + taps // 2
    share = rows // groups
    vmem = pl.BlockSpec(memory_space=pltpu.VMEM)
    anywhere = pl.BlockSpec(memory_space=pltpu.HBM)
    arguments = (
        records.reshape(shot_dev * rows * own_cols, samples),
        source_pattern,
        wavelet.T,
        filters.transpose(0, 2, 3, 1, 4).reshape(nref * taps, taps, 2, bin_total),
        vel_table,
        vel_index,
        freq_plan,
        counts,
    )
    arguments = tuple(pltpu.with_memory_space_constraint(a, pltpu.HBM) for a in arguments)
    scalars = (4, 6, 7)
    image = pl.pallas_call(
        functools.partial(kernel, dims),
        out_shape=jax.ShapeDtypeStruct((1, share, depth, cols), jnp.float32),
        in_specs=[anywhere] * len(arguments),
        out_specs=vmem,
        scratch_shapes=[
            (pltpu.SMEM if place in scalars else pltpu.VMEM)(array.shape, array.dtype)
            for place, array in enumerate(arguments)
        ] + [
            pltpu.VMEM((groups, planes, packs * SUB, LANES), jnp.bfloat16),
            pltpu.VMEM((groups, planes, packs * SUB, LANES), jnp.bfloat16),
            pltpu.VMEM((groups, planes, edge_packs * SUB, LANES), jnp.bfloat16),
            pltpu.VMEM((groups, planes, edge_packs * SUB, LANES), jnp.bfloat16),
            pltpu.VMEM(source_pattern.shape, source_pattern.dtype),
            pltpu.VMEM((lines * SEG, bin_total), jnp.bfloat16),
            pltpu.VMEM((planes, (taps + 1) // 2 * LANES, 2 * LANES), jnp.bfloat16),
            pltpu.VMEM((planes, row_pairs + margin, LANES // SLOT * SUB, LANES), jnp.bfloat16),
            pltpu.VMEM((planes, row_pairs, LANES // SLOT * SUB, LANES), jnp.bfloat16),
            pltpu.VMEM((rows, LANES), jnp.float32),
            pltpu.VMEM((groups, depth, share, LANES), jnp.float32),
            pltpu.VMEM((members, depth, share, LANES), jnp.float32),
            pltpu.SemaphoreType.DMA((len(arguments),)),
            pltpu.SemaphoreType.DMA((1,)),
            pltpu.SemaphoreType.DMA((planes,)),
            pltpu.SemaphoreType.DMA((1,)),
            pltpu.SemaphoreType.DMA((planes,)),
            pltpu.SemaphoreType.DMA((1,)),
            pltpu.SemaphoreType.DMA((1,)),
            pltpu.SemaphoreType.DMA((depth - 1, planes)),
            pltpu.SemaphoreType.DMA((depth - 1, planes)),
            pltpu.SemaphoreType.DMA((1,)),
            pltpu.SemaphoreType.DMA((1,)),
        ],
        compiler_params=pltpu.CompilerParams(
            collective_id=0, has_side_effects=True, vmem_limit_bytes=24 << 20
        ),
    )(*arguments)
    return image * scale


def solution(mesh):
    return jax.shard_map(
        body,
        mesh=mesh,
        in_specs=(
            P(("group", "shot"), "half", "freq", None),
            P(("group", "shot"), "half", None),
            P(),
            P(),
            P(),
            P("group", "half", None),
            P(),
            P(),
        ),
        out_specs=P("half", "freq", "group", None),
        check_vma=False,
    )
```
